32 devices in a mesh: fsdp: 8 (over z, x), rep: 4 (over y, core).
Axes of the slice: x: 2, y: 2, z: 4, core: 2. Of those that a mesh axis runs over, the one named last changes fastest.
Arguments:
- expert_base_rows: bfloat16 [4, 1536, 4096], P('rep', None, 'fsdp'), may hold values from -6 to 6
- factor_in: bfloat16 [4, 1536, 32], P('rep'), may hold values from -6 to 6
- factor_out: bfloat16 [4, 32, 4096], P('rep', None, 'fsdp'), may hold values from -0.29882812 to 0.29882812
- source_group: int32 [4], replicated, may hold values from 0 to 3
- tp_order: int32 [8], replicated, may hold values from 0 to 7, each once
Outputs:
- rollout_weights: bfloat16 [4, 4, 1536, 4096], P('rep', None, 'fsdp')
The draws below stay inside these ranges and needn't reach their ends.
Inputs may be any that keep to these rules, and one draw needn't show every extreme that they name: source_group[k] is the replica index along rep whose expert fills bucket k; entries may repeat. tp_order is a permutation of the 8 row blocks.
All inputs are finite; a program needn't handle non-finite values.
Results may differ from the reference program's by a relative error of at most 0.001.
Values may be sent and summed in bfloat16 or wider, within the bound.
A program may use at most 64 MiB of HBM per device.

```python
import jax
import jax.numpy as jnp
from jax import lax

D = 4096
FF = 1536
RANK = 32
PUB = 4
EXPERTS = 4
N_FSDP = 8
N_REP = 4


def set_ends(drawn, own_key, smallest, largest):
    place = [jax.random.randint(jax.random.fold_in(own_key, axis), (), 0, length) for axis, length in enumerate(drawn.shape)]
    widest = drawn.shape.index(max(drawn.shape))
    neighbour = place[:widest] + [(place[widest] + 1) % drawn.shape[widest]] + place[widest + 1:]
    return drawn.at[tuple(place)].set(smallest).at[tuple(neighbour)].set(largest)


def block_scale(stream_key, extent, split, least, largest):
    level, own = 1.0, jax.random.fold_in(stream_key, 6)
    for position, blocks in split:
        heights = jnp.exp(jax.random.uniform(jax.random.fold_in(own, position), (blocks,), jnp.float32, least / len(split), largest / len(split)))
        level = level * jnp.repeat(heights, extent[position] // blocks).reshape([-1 if axis == position else 1 for axis in range(len(extent))])
    return level


def noise(rng, extent, deviation, bound, pieces=(), kind=jnp.bfloat16):
    array = jax.random.normal(rng, extent, jnp.float32) * deviation
    if len(pieces) > 0:
        array = block_scale(rng, extent, pieces, -0.22, 0.18) * array
    return jnp.clip(array, min=-bound, max=bound).astype(kind)


def setup_inputs(seed: int = 0) -> dict:
    splits = jax.random.split(jax.random.key(seed), 6)
    return {
        "expert_base_rows": noise(splits[0], (EXPERTS, FF, D), 1.0, 6.0, ((0, 4), (2, 8))),
        "factor_in": noise(splits[1], (EXPERTS, FF, RANK), 1.0, 6.0, ((0, 4),)),
        "factor_out": noise(splits[2], (EXPERTS, RANK, D), 0.05, 0.29882812, ((0, 4), (2, 8))),
        "source_group": set_ends(jax.random.randint(splits[3], (PUB,), 0, N_REP), jax.random.fold_in(splits[3], 1), 0, N_REP - 1).astype(jnp.int32),
        "tp_order": jax.random.permutation(splits[4], N_FSDP).astype(jnp.int32),
    }


ADAPTER_SCALING = 2.0


def merge_expert(operands):
    weight_matrix, left_factor, right_factor = operands
    adapter_delta = jnp.dot(left_factor, right_factor, preferred_element_type=jnp.float32)
    return (weight_matrix.astype(jnp.float32) + ADAPTER_SCALING * adapter_delta).astype(jnp.bfloat16)


def reference(expert_base_rows, factor_in, factor_out, source_group, tp_order):
    merged_weight = lax.map(merge_expert, (expert_base_rows, factor_in, factor_out))
    chosen = jnp.take(merged_weight, source_group.astype(jnp.int32), axis=0)
    blocked = chosen.reshape(PUB, N_FSDP, FF // N_FSDP, D)
    ordered = jnp.take(blocked, tp_order.astype(jnp.int32), axis=1)
    published = ordered.reshape(PUB, FF, D)
    return jnp.broadcast_to(published[None], (N_REP, PUB, FF, D))
```

```python
import functools

import jax
import jax.numpy as jnp
from jax import lax
from jax.experimental import pallas as pl
from jax.experimental.pallas import tpu as pltpu
from jax.sharding import PartitionSpec as P

ADAPTER_SCALING = 2.0
GRANT = 16 * 1024 * 1024
MESH = pl.DeviceIdType.MESH


def flipped(position, step):
    for bit in range(step.bit_length()):
        if (step >> bit) & 1:
            weight = 1 << bit
            position = position + weight * (1 - 2 * ((position // weight) % 2))
    return position


def target(position, step, count):
    return flipped(position, step) if count & (count - 1) == 0 else (position + step) % count


def origin(position, step, count):
    return flipped(position, step) if count & (count - 1) == 0 else (position + count - step) % count


def merge_kernel(count, order_ref, base_ref, left_ref, right_ref, out_ref, merged):
    me = lax.axis_index("fsdp")
    rows = base_ref.shape[0] // count
    delta = lax.dot_general(
        left_ref[...], right_ref[...], (((0,), (0,)), ((), ())), preferred_element_type=jnp.float32
    )
    merged[...] = (base_ref[...].astype(jnp.float32) + ADAPTER_SCALING * delta).astype(merged.dtype)
    for step in range(count):
        block = order_ref[target(me, step, count)]
        out_ref[step] = merged[pl.ds(pl.multiple_of(block * rows, rows), rows), :]


def exchange_kernel(count, replicas, cores, group, halves, x_ref, g_ref, *sems):
    own_sem, a_send, a_recv, y_send, y_recv, c_send, c_recv = sems
    me, rep = lax.axis_index("fsdp"), lax.axis_index("rep")
    chips = replicas // cores
    chip, core = rep // cores, rep % cores
    partner = chip * cores + (cores - 1 - core)
    rows = x_ref.shape[1] // halves
    groups = count // group
    pieces = groups * halves

    peers = [(target(me, s, count), rep) for s in range(1, count)]
    peers += [(me, ((chip + d) % chips) * cores + core) for d in range(1, chips)]
    if cores == 2:
        peers += [(me, partner)]
    barrier = pltpu.get_barrier_semaphore()
    for peer in peers:
        pl.semaphore_signal(barrier, inc=1, device_id=peer, device_id_type=MESH)
    pl.semaphore_wait(barrier, len(peers))

    def send(src, dst, send_sem, recv_sem, peer):
        return pltpu.make_async_remote_copy(
            src_ref=src, dst_ref=dst, send_sem=send_sem, recv_sem=recv_sem, device_id=peer, device_id_type=MESH
        )

    def part(half):
        return pl.ds(half * rows, rows)

    started = []
    arriving = {}
    keep = pltpu.make_async_copy(x_ref.at[0], g_ref.at[rep, 0], own_sem)
    keep.start()

    def exchange(step, half):
        copy = send(
            x_ref.at[step, part(half)], g_ref.at[rep, step, part(half)],
            a_send.at[step * halves + half], a_recv.at[step * halves + half],
            (target(me, step, count), rep),
        )
        copy.start()
        arriving[step, half] = copy

    def plane(index, number, half):
        return g_ref.at[index, pl.ds(number * group, group), part(half)]

    across = {}

    def forward(number, half):
        piece = number * halves + half
        own = group == 1 and number == 0
        src = x_ref.at[pl.ds(0, 1), part(half)] if own else plane(rep, number, half)
        dst = plane(rep, number, half)
        for d in range(1, chips):
            at = (d - 1) * pieces + piece
            copy = send(src, dst, y_send.at[at], y_recv.at[at], (me, ((chip + d) % chips) * cores + core))
            copy.start()
            across[d, number, half] = copy
        if cores == 2:
            copy = send(src, dst, c_send.at[piece], c_recv.at[piece], (me, partner))
            copy.start()
            started.append(copy)

    def relay(number, half):
        piece = number * halves + half
        for d in range(1, chips):
            across[d, number, half].wait_recv()
            if cores == 2:
                came = plane(((chip + chips - d) % chips) * cores + core, number, half)
                at = d * pieces + piece
                copy = send(came, came, c_send.at[at], c_recv.at[at], (me, partner))
                copy.start()
                started.append(copy)

    order = [(number, half) for number in range(groups) for half in range(halves)]
    lag = halves
    if group == 1:
        for half in range(halves):
            forward(0, half)
    for step in range(1, count):
        for half in range(halves):
            exchange(step, half)
    if group > 1:
        keep.wait()
    for at, (number, half) in enumerate(order):
        for step in range(max(1, number * group), (number + 1) * group):
            arriving[step, half].wait_recv()
        if group > 1 or number > 0:
            forward(number, half)
        if at >= lag:
            relay(*order[at - lag])
    for number, half in order[len(order) - lag:]:
        relay(number, half)
    for copy in started:
        copy.wait()
    for copy in across.values():
        copy.wait_send()
    for copy in arriving.values():
        copy.wait_send()
    if group == 1:
        keep.wait()


def select_kernel(count, source_ref, g_ref, out_ref, sems):
    me = lax.axis_index("fsdp")
    width = g_ref.shape[3]
    copies = []
    for bucket in range(out_ref.shape[0]):
        for step in range(count):
            columns = pl.ds(pl.multiple_of(origin(me, step, count) * width, width), width)
            copy = pltpu.make_async_copy(
                g_ref.at[source_ref[bucket], step], out_ref.at[bucket, :, columns], sems.at[bucket, step]
            )
            copy.start()
            copies.append(copy)
    for copy in copies:
        copy.wait()


def body(expert_base_rows, factor_in, factor_out, source_group, tp_order):
    count, replicas = lax.axis_size("fsdp"), lax.axis_size("rep")
    hidden, width = expert_base_rows.shape[1:]
    rows = hidden // count
    buckets = source_group.shape[0]
    cores = 2 if replicas % 2 == 0 else 1
    chips = replicas // cores
    group = max(1, count // 8) if count % 8 == 0 else 1
    halves = 2 if group == 1 and rows % 32 == 0 else 1
    pieces = count // group * halves
    vmem, smem, anywhere = (pl.BlockSpec(memory_space=m) for m in (pltpu.VMEM, pltpu.SMEM, pl.ANY))
    kind = expert_base_rows.dtype

    blocks = pl.pallas_call(
        functools.partial(merge_kernel, count),
        out_shape=pltpu.VMEM((count, rows, width), kind),
        in_specs=[smem, vmem, vmem, vmem],
        out_specs=vmem,
        scratch_shapes=[pltpu.VMEM((hidden, width), kind)],
        compiler_params=pltpu.CompilerParams(vmem_limit_bytes=GRANT),
        name="merge",
    )(tp_order, expert_base_rows[0], factor_in[0].T, factor_out[0])

    dma = pltpu.SemaphoreType.DMA
    planes = pl.pallas_call(
        functools.partial(exchange_kernel, count, replicas, cores, group, halves),
        out_shape=pltpu.VMEM((replicas, count, rows, width), kind),
        in_specs=[vmem],
        out_specs=vmem,
        scratch_shapes=[
            dma,
            dma((count * halves,)), dma((count * halves,)),
            dma((max(1, chips - 1) * pieces,)), dma((max(1, chips - 1) * pieces,)),
            dma((chips * pieces,)), dma((chips * pieces,)),
        ],
        compiler_params=pltpu.CompilerParams(collective_id=0, has_side_effects=True, vmem_limit_bytes=GRANT),
        name="exchange",
    )(blocks)

    out = pl.pallas_call(
        functools.partial(select_kernel, count),
        out_shape=jax.ShapeDtypeStruct((buckets, rows, count * width), kind),
        in_specs=[smem, vmem],
        out_specs=anywhere,
        scratch_shapes=[dma((buckets, count))],
        compiler_params=pltpu.CompilerParams(vmem_limit_bytes=GRANT),
        name="select",
    )(source_group, planes)
    return out[None]


def solution(mesh):
    placed = (P("rep", None, "fsdp"), P("rep", None, None), P("rep", None, "fsdp"), P(), P())
    return jax.shard_map(
        body, mesh=mesh, in_specs=placed, out_specs=P("rep", None, "fsdp", None), check_vma=False
    )
```

```python
import functools

import jax
import jax.numpy as jnp
from jax import lax
from jax.experimental import pallas as pl
from jax.experimental.pallas import tpu as pltpu
from jax.sharding import PartitionSpec as P

ADAPTER_SCALING = 2.0
GRANT = 16 * 1024 * 1024
MESH = pl.DeviceIdType.MESH


def flipped(position, step):
    for bit in range(step.bit_length()):
        if (step >> bit) & 1:
            weight = 1 << bit
            position = position + weight * (1 - 2 * ((position // weight) % 2))
    return position


def target(position, step, count):
    return flipped(position, step) if count & (count - 1) == 0 else (position + step) % count


def origin(position, step, count):
    return flipped(position, step) if count & (count - 1) == 0 else (position + count - step) % count


def exchange_kernel(
    count, replicas, cores, group, halves,
    order_in, base_in, left_in, right_in, g_ref, order_ref, base_ref, left_ref, right_ref, merged, x_ref, *sems
):
    load_sems, own_sem, a_send, a_recv, y_send, y_recv, c_send, c_recv = sems
    loads = [
        pltpu.make_async_copy(src, dst, load_sems.at[at])
        for at, (src, dst) in enumerate(
            ((left_in, left_ref), (right_in, right_ref), (order_in, order_ref), (base_in, base_ref))
        )
    ]
    for load in loads:
        load.start()
    me, rep = lax.axis_index("fsdp"), lax.axis_index("rep")
    chips = replicas // cores
    chip, core = rep // cores, rep % cores
    partner = chip * cores + (cores - 1 - core)
    rows = x_ref.shape[1] // halves
    groups = count // group
    pieces = groups * halves

    peers = [(target(me, s, count), rep) for s in range(1, count)]
    peers += [(me, ((chip + d) % chips) * cores + core) for d in range(1, chips)]
    if cores == 2:
        peers += [(me, partner)]
    barrier = pltpu.get_barrier_semaphore()
    for peer in peers:
        pl.semaphore_signal(barrier, inc=1, device_id=peer, device_id_type=MESH)

    loads[0].wait()
    loads[1].wait()
    delta = lax.dot_general(
        left_ref[...], right_ref[...], (((0,), (0,)), ((), ())), preferred_element_type=jnp.float32
    )
    loads[2].wait()
    loads[3].wait()
    total = base_ref[...].astype(jnp.float32) + ADAPTER_SCALING * delta
    merged[...] = total.astype(merged.dtype).reshape(merged.shape)
    for step in range(count):
        x_ref[step] = merged[order_ref[target(me, step, count)]]
    pl.semaphore_wait(barrier, len(peers))

    def send(src, dst, send_sem, recv_sem, peer):
        return pltpu.make_async_remote_copy(
            src_ref=src, dst_ref=dst, send_sem=send_sem, recv_sem=recv_sem, device_id=peer, device_id_type=MESH
        )

    def part(half):
        return pl.ds(half * rows, rows)

    started = []
    arriving = {}
    keep = pltpu.make_async_copy(x_ref.at[0], g_ref.at[rep, 0], own_sem)
    keep.start()

    def exchange(step, half):
        copy = send(
            x_ref.at[step, part(half)], g_ref.at[rep, step, part(half)],
            a_send.at[step * halves + half], a_recv.at[step * halves + half],
            (target(me, step, count), rep),
        )
        copy.start()
        arriving[step, half] = copy

    def plane(index, number, half):
        return g_ref.at[index, pl.ds(number * group, group), part(half)]

    across = {}

    def forward(number, half):
        piece = number * halves + half
        own = group == 1 and number == 0
        src = x_ref.at[pl.ds(0, 1), part(half)] if own else plane(rep, number, half)
        dst = plane(rep, number, half)
        for d in range(1, chips):
            at = (d - 1) * pieces + piece
            copy = send(src, dst, y_send.at[at], y_recv.at[at], (me, ((chip + d) % chips) * cores + core))
            copy.start()
            across[d, number, half] = copy
        if cores == 2:
            copy = send(src, dst, c_send.at[piece], c_recv.at[piece], (me, partner))
            copy.start()
            started.append(copy)

    def relay(number, half):
        piece = number * halves + half
        for d in range(1, chips):
            across[d, number, half].wait_recv()
            if cores == 2:
                came = plane(((chip + chips - d) % chips) * cores + core, number, half)
                at = d * pieces + piece
                copy = send(came, came, c_send.at[at], c_recv.at[at], (me, partner))
                copy.start()
                started.append(copy)

    order = [(number, half) for number in range(groups) for half in range(halves)]
    lag = halves
    if group == 1:
        for half in range(halves):
            forward(0, half)
    for step in range(1, count):
        for half in range(halves):
            exchange(step, half)
    if group > 1:
        keep.wait()
    for at, (number, half) in enumerate(order):
        for step in range(max(1, number * group), (number + 1) * group):
            arriving[step, half].wait_recv()
        if group > 1 or number > 0:
            forward(number, half)
        if at >= lag:
            relay(*order[at - lag])
    for number, half in order[len(order) - lag:]:
        relay(number, half)
    for copy in started:
        copy.wait()
    for copy in across.values():
        copy.wait_send()
    for copy in arriving.values():
        copy.wait_send()
    if group == 1:
        keep.wait()


def select_kernel(count, source_ref, g_ref, out_ref, sems):
    me = lax.axis_index("fsdp")
    width = g_ref.shape[3]
    copies = []
    for bucket in range(out_ref.shape[0]):
        for step in range(count):
            columns = pl.ds(pl.multiple_of(origin(me, step, count) * width, width), width)
            copy = pltpu.make_async_copy(
                g_ref.at[source_ref[bucket], step], out_ref.at[bucket, :, columns], sems.at[bucket, step]
            )
            copy.start()
            copies.append(copy)
    for copy in copies:
        copy.wait()


def body(expert_base_rows, factor_in, factor_out, source_group, tp_order):
    count, replicas = lax.axis_size("fsdp"), lax.axis_size("rep")
    hidden, width = expert_base_rows.shape[1:]
    rows = hidden // count
    buckets = source_group.shape[0]
    cores = 2 if replicas % 2 == 0 else 1
    chips = replicas // cores
    group = max(1, count // 8) if count % 8 == 0 else 1
    halves = 2 if group == 1 and rows % 32 == 0 else 1
    pieces = count // group * halves
    vmem, smem, hbm, anywhere = (
        pl.BlockSpec(memory_space=m) for m in (pltpu.VMEM, pltpu.SMEM, pltpu.HBM, pl.ANY)
    )
    kind = expert_base_rows.dtype

    left, right = factor_in[0].T, factor_out[0]
    dma = pltpu.SemaphoreType.DMA
    planes = pl.pallas_call(
        functools.partial(exchange_kernel, count, replicas, cores, group, halves),
        out_shape=pltpu.VMEM((replicas, count, rows, width), kind),
        in_specs=[hbm] * 4,
        out_specs=vmem,
        scratch_shapes=[
            pltpu.SMEM(tp_order.shape, tp_order.dtype),
            pltpu.VMEM((hidden, width), kind),
            pltpu.VMEM(left.shape, kind),
            pltpu.VMEM(right.shape, kind),
            pltpu.VMEM((count, rows, width), kind),
            pltpu.VMEM((count, rows, width), kind),
            dma((4,)), dma,
            dma((count * halves,)), dma((count * halves,)),
            dma((max(1, chips - 1) * pieces,)), dma((max(1, chips - 1) * pieces,)),
            dma((chips * pieces,)), dma((chips * pieces,)),
        ],
        compiler_params=pltpu.CompilerParams(collective_id=0, has_side_effects=True, vmem_limit_bytes=GRANT),
        name="exchange",
    )(*(pltpu.with_memory_space_constraint(a, pltpu.HBM) for a in (tp_order, expert_base_rows[0], left, right)))

    out = pl.pallas_call(
        functools.partial(select_kernel, count),
        out_shape=jax.ShapeDtypeStruct((buckets, rows, count * width), kind),
        in_specs=[smem, vmem],
        out_specs=anywhere,
        scratch_shapes=[dma((buckets, count))],
        compiler_params=pltpu.CompilerParams(vmem_limit_bytes=GRANT),
        name="select",
    )(source_group, planes)
    return out[None]


def solution(mesh):
    placed = (P("rep", None, "fsdp"), P("rep", None, None), P("rep", None, "fsdp"), P(), P())
    return jax.shard_map(
        body, mesh=mesh, in_specs=placed, out_specs=P("rep", None, "fsdp", None), check_vma=False
    )
```

```python
import functools

import jax
import jax.numpy as jnp
from jax import lax
from jax.experimental import pallas as pl
from jax.experimental.pallas import tpu as pltpu
from jax.sharding import PartitionSpec as P

ADAPTER_SCALING = 2.0
GRANT = 40 * 1024 * 1024
MESH = pl.DeviceIdType.MESH


def flipped(position, step):
    for bit in range(step.bit_length()):
        if (step >> bit) & 1:
            weight = 1 << bit
            position = position + weight * (1 - 2 * ((position // weight) % 2))
    return position


def target(position, step, count):
    return flipped(position, step) if count & (count - 1) == 0 else (position + step) % count


def origin(position, step, count):
    return flipped(position, step) if count & (count - 1) == 0 else (position + count - step) % count


def exchange_kernel(
    count, replicas, cores, group, halves,
    source_in, order_in, base_in, left_in, right_in, out_ref,
    source_ref, order_ref, base_ref, left_ref, right_ref, merged, x_ref, *rest
):
    planes, sems = rest[: count // group], rest[count // group:]
    load_sems, own_sem, a_send, a_recv, y_send, y_recv, c_send, c_recv = sems
    loads = [
        pltpu.make_async_copy(src, dst, load_sems.at[at])
        for at, (src, dst) in enumerate(
            ((left_in, left_ref), (right_in, right_ref), (order_in, order_ref), (base_in, base_ref),
             (source_in, source_ref))
        )
    ]
    for load in loads:
        load.start()
    me, rep = lax.axis_index("fsdp"), lax.axis_index("rep")
    chips = replicas // cores
    chip, core = rep // cores, rep % cores
    partner = chip * cores + (cores - 1 - core)
    rows = x_ref.shape[1] // halves
    groups = count // group
    pieces = groups * halves

    peers = [(target(me, s, count), rep) for s in range(1, count)]
    peers += [(me, ((chip + d) % chips) * cores + core) for d in range(1, chips)]
    if cores == 2:
        peers += [(me, partner)]
    barrier = pltpu.get_barrier_semaphore()
    for peer in peers:
        pl.semaphore_signal(barrier, inc=1, device_id=peer, device_id_type=MESH)

    loads[0].wait()
    loads[1].wait()
    delta = lax.dot_general(
        left_ref[...], right_ref[...], (((0,), (0,)), ((), ())), preferred_element_type=jnp.float32
    )
    loads[2].wait()
    loads[3].wait()
    loads[4].wait()
    total = base_ref[...].astype(jnp.float32) + ADAPTER_SCALING * delta
    merged[...] = total.astype(merged.dtype).reshape(merged.shape)
    for step in range(count):
        x_ref[step] = merged[order_ref[target(me, step, count)]]
    pl.semaphore_wait(barrier, len(peers))

    def send(src, dst, send_sem, recv_sem, peer):
        return pltpu.make_async_remote_copy(
            src_ref=src, dst_ref=dst, send_sem=send_sem, recv_sem=recv_sem, device_id=peer, device_id_type=MESH
        )

    def part(half):
        return pl.ds(half * rows, rows)

    crossing = {}
    arriving = {}
    keep = pltpu.make_async_copy(x_ref.at[0], planes[0].at[rep, 0], own_sem)
    keep.start()

    def exchange(step, half):
        copy = send(
            x_ref.at[step, part(half)], planes[step // group].at[rep, step % group, part(half)],
            a_send.at[step * halves + half], a_recv.at[step * halves + half],
            (target(me, step, count), rep),
        )
        copy.start()
        arriving[step, half] = copy

    def plane(index, number, half):
        return planes[number].at[index, :, part(half)]

    across = {}

    def forward(number, half):
        piece = number * halves + half
        own = group == 1 and number == 0
        src = x_ref.at[pl.ds(0, 1), part(half)] if own else plane(rep, number, half)
        dst = plane(rep, number, half)
        for d in range(1, chips):
            at = (d - 1) * pieces + piece
            copy = send(src, dst, y_send.at[at], y_recv.at[at], (me, ((chip + d) % chips) * cores + core))
            copy.start()
            across[d, number, half] = copy
        if cores == 2:
            copy = send(src, dst, c_send.at[piece], c_recv.at[piece], (me, partner))
            copy.start()
            crossing[0, number, half] = copy

    def relay(number, half):
        piece = number * halves + half
        for d in range(1, chips):
            across[d, number, half].wait_recv()
            if cores == 2:
                came = plane(((chip + chips - d) % chips) * cores + core, number, half)
                at = d * pieces + piece
                copy = send(came, came, c_send.at[at], c_recv.at[at], (me, partner))
                copy.start()
                crossing[d, number, half] = copy

    def finish(number):
        if number == 0 and group == 1:
            keep.wait()
        if cores == 2:
            for d in range(chips):
                for half in range(halves):
                    crossing[d, number, half].wait_recv()
        width = x_ref.shape[2]
        for slot in range(group):
            first = pl.multiple_of(origin(me, number * group + slot, count) * width, width)
            for bucket in range(out_ref.shape[0]):
                out_ref[bucket, :, pl.ds(first, width)] = planes[number][source_ref[bucket], slot]

    order = [(number, half) for number in range(groups) for half in range(halves)]
    lag = 2 * halves
    if group == 1:
        for half in range(halves):
            forward(0, half)
    for step in range(1, count):
        for half in range(halves):
            exchange(step, half)
    if group > 1:
        keep.wait()
    for at in range(len(order) + 2 * lag):
        if at < len(order):
            number, half = order[at]
            for step in range(max(1, number * group), (number + 1) * group):
                arriving[step, half].wait_recv()
            if group > 1 or number > 0:
                forward(number, half)
        if 0 <= at - lag < len(order):
            relay(*order[at - lag])
        if 0 <= at - 2 * lag < len(order):
            number, half = order[at - 2 * lag]
            if half == halves - 1:
                finish(number)
    for copy in (*crossing.values(), *across.values(), *arriving.values()):
        copy.wait_send()


def body(expert_base_rows, factor_in, factor_out, source_group, tp_order):
    count, replicas = lax.axis_size("fsdp"), lax.axis_size("rep")
    hidden, width = expert_base_rows.shape[1:]
    rows = hidden // count
    cores = 2 if replicas % 2 == 0 else 1
    chips = replicas // cores
    group = max(1, count // 8) if count % 8 == 0 else 1
    halves = 2 if group == 1 and rows % 32 == 0 else 1
    pieces = count // group * halves
    kind = expert_base_rows.dtype

    left, right = factor_in[0].T, factor_out[0]
    dma = pltpu.SemaphoreType.DMA
    whole = functools.partial(pltpu.with_memory_space_constraint, memory_space=pltpu.HBM)
    out = pl.pallas_call(
        functools.partial(exchange_kernel, count, replicas, cores, group, halves),
        out_shape=pltpu.VMEM((source_group.shape[0], rows, count * width), kind),
        in_specs=[pl.BlockSpec(memory_space=pltpu.HBM)] * 5,
        out_specs=pl.BlockSpec(memory_space=pltpu.VMEM),
        scratch_shapes=[
            pltpu.SMEM(source_group.shape, source_group.dtype),
            pltpu.SMEM(tp_order.shape, tp_order.dtype),
            pltpu.VMEM((hidden, width), kind),
            pltpu.VMEM(left.shape, kind),
            pltpu.VMEM(right.shape, kind),
            pltpu.VMEM((count, rows, width), kind),
            pltpu.VMEM((count, rows, width), kind),
            *[pltpu.VMEM((replicas, group, rows, width), kind)] * (count // group),
            dma((5,)), dma,
            dma((count * halves,)), dma((count * halves,)),
            dma((max(1, chips - 1) * pieces,)), dma((max(1, chips - 1) * pieces,)),
            dma((chips * pieces,)), dma((chips * pieces,)),
        ],
        compiler_params=pltpu.CompilerParams(collective_id=0, has_side_effects=True, vmem_limit_bytes=GRANT),
        name="exchange",
    )(*map(whole, (source_group, tp_order, expert_base_rows[0], left, right)))
    return out[None]


def solution(mesh):
    placed = (P("rep", None, "fsdp"), P("rep", None, None), P("rep", None, "fsdp"), P(), P())
    return jax.shard_map(
        body, mesh=mesh, in_specs=placed, out_specs=P("rep", None, "fsdp", None), check_vma=False
    )
```
